32 devices in a mesh: dp: 8 (over z, y), tm: 4 (over x, core).
Axes of the slice: x: 2, y: 2, z: 4, core: 2. Of those that a mesh axis runs over, the one named last changes fastest.
Arguments:
- mel: float32 [16, 1024, 80], P('dp', 'tm'), may hold values from -6 to 6
- cotangent: float32 [16, 1024, 80], P('dp', 'tm'), may hold values from -6 to 6
- lengths: int32 [16], P('dp'), may hold values from 1 to 1024, 9830 in all
- w_first: float32 [5, 80, 512], replicated, may hold values from -0.3125 to 0.3125
- w_mid: float32 [3, 5, 512, 512], replicated, may hold values from -0.125 to 0.125
- w_last: float32 [5, 512, 80], replicated, may hold values from -0.125 to 0.125
- gain_hidden: float32 [4, 512], replicated, may hold values from 0.5 to 1.5
- bias_hidden: float32 [4, 512], replicated, may hold values from -3 to 3
- gain_last: float32 [80], replicated, may hold values from 0.5 to 1.5
- bias_last: float32 [80], replicated, may hold values from -3 to 3
Outputs:
- mel_after: float32 [16, 1024, 80], P('dp', 'tm')
- grad_mel: float32 [16, 1024, 80], P('dp', 'tm')
- grad_w_first: float32 [5, 80, 512], replicated
- grad_w_mid: float32 [3, 5, 512, 512], replicated
- grad_w_last: float32 [5, 512, 80], replicated
- grad_gain_hidden: float32 [4, 512], replicated
- grad_bias_hidden: float32 [4, 512], replicated
- grad_gain_last: float32 [80], replicated
- grad_bias_last: float32 [80], replicated
The draws below stay inside these ranges and needn't reach their ends.
Inputs may be any that keep to these rules, and one draw needn't show every extreme that they name: `lengths`: each utterance has at least one frame; in every draw some utterance fills all 1024 frame slots.
All inputs are finite; a program needn't handle non-finite values. No bound on the sum of `lengths` on one device may be relied on, other than what follows from the above.
Results may differ from the reference program's by a relative error of at most 0.00029.
Values sent between devices are 32-bit elements; how exact they have to be, the bound alone decides.
No kernel may reach another device: no remote copies, remote signals or barrier semaphores. Data moves between devices by JAX's collectives and lax.ppermute only.
A program may use at most 192 MiB of HBM per device.

```python
import math
import jax
import jax.numpy as jnp
import numpy as np
from jax import lax

C = 512
MEL = 80
KW = 5
L = 1024
BATCH = 16


def block_levels(rng, dims, shards, least, largest):
    factor_of, own = 1.0, jax.random.fold_in(rng, 6)
    for axis_at, blocks in shards:
        draws = jnp.exp(jax.random.uniform(jax.random.fold_in(own, axis_at), (blocks,), jnp.float32, least / len(shards), largest / len(shards)))
        factor_of = factor_of * jnp.repeat(draws, dims[axis_at] // blocks).reshape([-1 if axis == axis_at else 1 for axis in range(len(dims))])
    return factor_of


def profile(amount, total, bound, slope):
    weights = [(1 << 20) // math.isqrt(grade ** slope) + 1 for grade in range(2, amount + 1)]
    surplus, given = total - bound - (amount - 1), [1] * (amount - 1)
    while surplus > 0:
        movable = [i for i in range(amount - 1) if given[i] < bound]
        pool, left = sum([weights[i] for i in movable]), surplus
        for i in movable:
            extra = min(bound - given[i], max(1, left * weights[i] // pool), surplus)
            given[i] = given[i] + extra
            surplus = surplus - extra
    return np.array([bound] + given)


def uneven_parts(rng, number_of, total, bound, slope):
    if number_of == 2:
        one = jax.random.randint(rng, (), max(1, total - bound), min(bound, total - 1) + 1)
        return jnp.stack([one, total - one])
    sizes = jnp.asarray(profile(number_of, total, bound, slope), jnp.int32)
    twos = (number_of - 1) // 2
    donor, sink = sizes[1:1 + 2 * twos:2], sizes[2:2 + 2 * twos:2]
    slack = jnp.minimum(donor - 1, bound - sink)
    moved = jax.random.randint(jax.random.fold_in(rng, 1), (twos,), 0, 1 << 20) % (slack + 1)
    sizes = sizes.at[1:1 + 2 * twos:2].set(donor - moved).at[2:2 + 2 * twos:2].set(sink + moved)
    return sizes[jax.random.permutation(jax.random.fold_in(rng, 2), number_of)]


def noise(own_key, shape, deviation, most, pieces=(), held_as=jnp.bfloat16):
    result = jax.random.normal(own_key, shape, jnp.float32) * deviation
    if len(pieces) > 0:
        result = block_levels(own_key, shape, pieces, -0.22, 0.18) * result
    return jnp.clip(result, min=-most, max=most).astype(held_as)


def setup_inputs(seed: int = 0) -> dict:
    keys = jax.random.split(jax.random.key(seed), 11)
    return {
        "mel": noise(keys[0], (BATCH, L, MEL), 1.0, 6.0, ((0, 8), (1, 4)), jnp.float32),
        "cotangent": noise(keys[1], (BATCH, L, MEL), 1.0, 6.0, ((0, 8), (1, 4)), jnp.float32),
        "lengths": uneven_parts(keys[2], BATCH, BATCH * L * 3 // 5, L, 2).astype(jnp.int32),
        "w_first": noise(keys[3], (KW, MEL, C), (KW * MEL) ** -0.5, 0.3125, (), jnp.float32),
        "w_mid": noise(keys[4], (3, KW, C, C), (KW * C) ** -0.5, 0.125, (), jnp.float32),
        "w_last": noise(keys[5], (KW, C, MEL), (KW * C) ** -0.5, 0.125, (), jnp.float32),
        "gain_hidden": jnp.clip(1.0 + 0.1 * jax.random.normal(keys[6], (4, C), jnp.float32), 0.5, 1.5),
        "bias_hidden": noise(keys[7], (4, C), 0.5, 3.0, (), jnp.float32),
        "gain_last": jnp.clip(1.0 + 0.1 * jax.random.normal(keys[8], (MEL,), jnp.float32), 0.5, 1.5),
        "bias_last": noise(keys[9], (MEL,), 0.5, 3.0, (), jnp.float32),
    }


def convolve(x, w):
    frames = x.shape[1]
    padded = jnp.pad(x, ((0, 0), (2, 2), (0, 0)))
    total = jnp.zeros(x.shape[:2] + (w.shape[2],), jnp.float32)
    for k in range(w.shape[0]):
        total = total + jnp.einsum('btc,cd->btd', padded[:, k:k + frames], w[k], precision=lax.Precision.HIGHEST)
    return total

def reference(mel, cotangent, lengths, w_first, w_mid, w_last, gain_hidden, bias_hidden, gain_last, bias_last):
    frames = mel.shape[1]
    position = jnp.arange(frames, dtype=jnp.int32)
    mask = (position[None, :] < lengths[:, None]).astype(jnp.float32)[:, :, None]
    count = jnp.sum(mask)

    def forward(mel_in, wf, wm, wl, gh, bh, gl, bl):
        weights = [wf, wm[0], wm[1], wm[2], wl]
        gains = [gh[0], gh[1], gh[2], gh[3], gl]
        shifts = [bh[0], bh[1], bh[2], bh[3], bl]
        x = mel_in
        for layer in range(5):
            h = convolve(x, weights[layer])
            mean = lax.optimization_barrier(jnp.sum(mask * h, axis=(0, 1))) / count
            var = lax.optimization_barrier(jnp.sum(mask * h * h, axis=(0, 1))) / count - mean * mean
            z = (h - mean) * lax.rsqrt(var + 1e-05) * gains[layer] + shifts[layer]
            if layer < 4:
                x = mask * jnp.tanh(z)
            else:
                x = mask * z
        return mel_in + x
    out, pullback = jax.vjp(forward, mel, w_first, w_mid, w_last, gain_hidden, bias_hidden, gain_last, bias_last)
    grads = pullback(cotangent)
    return (out, grads[0], grads[1], grads[2], grads[3], grads[4], grads[5], grads[6], grads[7])
```

```python
import jax
import jax.numpy as jnp
from jax import lax
from jax.sharding import PartitionSpec as P

AXES = ("dp", "tm")
EDGE = 24
HIGH = lax.Precision.HIGH


def extend(block):
    count = lax.axis_size("tm")
    forward = [(i, i + 1) for i in range(count - 1)]
    backward = [(j, i) for i, j in forward]
    low = lax.ppermute(block[:, -EDGE:], "tm", forward)
    high = lax.ppermute(block[:, :EDGE], "tm", backward)
    return jnp.concatenate([low, block, high], axis=1)


def all_sum(parts):
    devices = lax.axis_size(AXES)
    copies = jnp.broadcast_to(parts[None], (devices,) + parts.shape)
    return jnp.sum(lax.all_to_all(copies, AXES, 0, 0), axis=0)


def shifted(x, width):
    rows = x.shape[0]
    padded = jnp.pad(x, ((width // 2, width // 2), (0, 0)))
    return jnp.concatenate([padded[k : k + rows] for k in range(width)], axis=1)


def shards(
    mel, cotangent, lengths, w_first, w_mid, w_last, gain_hidden, bias_hidden, gain_last, bias_last
):
    batch, frames, mels = mel.shape
    width = w_first.shape[0]
    span = frames + 2 * EDGE
    rows = batch * span
    both = extend(jnp.concatenate([mel, cotangent], axis=2)).reshape(rows, 2 * mels)
    mel_ext, cot_ext = both[:, :mels], both[:, mels:]
    local = jnp.arange(span, dtype=jnp.int32) - EDGE
    position = lax.axis_index("tm") * frames + local
    live = (position[None, :] >= 0) & (position[None, :] < lengths[:, None])
    mask = live.astype(jnp.float32).reshape(rows, 1)
    inside = (local >= 0) & (local < frames)
    own = (live & inside[None, :]).astype(jnp.float32).reshape(rows, 1)
    local_count = jnp.sum(own)
    weights = [w_first, w_mid[0], w_mid[1], w_mid[2], w_last]
    gains = [gain_hidden[0], gain_hidden[1], gain_hidden[2], gain_hidden[3], gain_last]
    shifts = [bias_hidden[0], bias_hidden[1], bias_hidden[2], bias_hidden[3], bias_last]
    kept = []
    count = None
    x = mel_ext
    last_sums = None
    for layer in range(5):
        weight = weights[layer]
        x_wide = shifted(x, width)
        h = jnp.dot(x_wide, weight.reshape(-1, weight.shape[2]), precision=HIGH)
        masked = own * h
        sums = [jnp.sum(masked, axis=0), jnp.sum(masked * h, axis=0)]
        if layer == 0:
            sums.append(jnp.broadcast_to(local_count, sums[0].shape))
        if layer == 4:
            sums += [jnp.sum(own * cot_ext, axis=0), jnp.sum(masked * cot_ext, axis=0)]
        sums = all_sum(jnp.stack(sums))
        if layer == 0:
            count = sums[2, 0]
        mean = sums[0] / count
        rstd = lax.rsqrt(sums[1] / count - mean * mean + 1e-05)
        normed = (h - mean) * rstd
        z_value = normed * gains[layer] + shifts[layer]
        if layer < 4:
            active = jnp.tanh(z_value)
            x = mask * active
        else:
            active = None
            x = mask * z_value
            last_sums = (rstd * (sums[3] - mean * sums[2]), sums[2])
        kept.append((x_wide, normed, rstd, active))

    def unextend(block):
        return block.reshape(batch, span, mels)[:, EDGE : EDGE + frames]

    mel_after = mel + unextend(x)
    grad = cot_ext
    weight_grads = [None] * 5
    gain_grads = [None] * 5
    shift_grads = [None] * 5
    for layer in range(4, -1, -1):
        x_wide, normed, rstd, active = kept[layer]
        weight = weights[layer]
        gz = grad * mask
        if layer < 4:
            gz = gz * (1.0 - active * active)
            mine = own * gz
            sums = all_sum(jnp.stack([jnp.sum(mine * normed, axis=0), jnp.sum(mine, axis=0)]))
            d_gain, d_shift = sums[0], sums[1]
        else:
            d_gain, d_shift = last_sums
        gain_grads[layer] = d_gain
        shift_grads[layer] = d_shift
        d_pre = mask * rstd * gains[layer] * (gz - d_shift / count - normed * d_gain / count)
        weight_grads[layer] = jnp.dot(x_wide.T, own * d_pre, precision=HIGH)
        flipped = jnp.transpose(weight[::-1], (0, 2, 1)).reshape(-1, weight.shape[1])
        grad = jnp.dot(shifted(d_pre, width), flipped, precision=HIGH)
    grad_mel = cotangent + unextend(grad)
    weight_grads = lax.psum(weight_grads, AXES)
    grad_w_mid = jnp.stack([weight_grads[i].reshape(w_mid.shape[1:]) for i in (1, 2, 3)])
    return (
        mel_after,
        grad_mel,
        weight_grads[0].reshape(w_first.shape),
        grad_w_mid,
        weight_grads[4].reshape(w_last.shape),
        jnp.stack(gain_grads[:4]),
        jnp.stack(shift_grads[:4]),
        gain_grads[4],
        shift_grads[4],
    )


def solution(mesh):
    return jax.shard_map(
        shards,
        mesh=mesh,
        in_specs=(P("dp", "tm", None), P("dp", "tm", None), P("dp")) + (P(),) * 7,
        out_specs=(P("dp", "tm", None), P("dp", "tm", None)) + (P(),) * 7,
        check_vma=False,
    )
```

```python
import jax
import jax.numpy as jnp
from jax import lax
from jax.sharding import PartitionSpec as P

AXES = ("dp", "tm")
EDGE = 24
HIGH = lax.Precision.HIGH


def extend(block):
    count = lax.axis_size("tm")
    forward = [(i, i + 1) for i in range(count - 1)]
    backward = [(j, i) for i, j in forward]
    low = lax.ppermute(block[:, -EDGE:], "tm", forward)
    high = lax.ppermute(block[:, :EDGE], "tm", backward)
    return jnp.concatenate([low, block, high], axis=1)


def all_sum(parts):
    devices = lax.axis_size(AXES)
    copies = jnp.broadcast_to(parts[None], (devices,) + parts.shape)
    return jnp.sum(lax.all_to_all(copies, AXES, 0, 0), axis=0)


def swap(x, bit):
    devices = lax.axis_size(AXES)
    return lax.ppermute(x, AXES, [(i, i ^ (1 << bit)) for i in range(devices)])


def halve(x, bit):
    half = x.shape[0] // 2
    upper = ((lax.axis_index(AXES) >> bit) & 1) == 1
    low, high = x[:half], x[half:]
    return jnp.where(upper, high, low) + swap(jnp.where(upper, low, high), bit)


def double(x, bit):
    upper = ((lax.axis_index(AXES) >> bit) & 1) == 1
    other = swap(x, bit)
    return jnp.concatenate([jnp.where(upper, other, x), jnp.where(upper, x, other)], axis=0)


def exchange_sum(x, sizes):
    bits = (lax.axis_size(AXES) - 1).bit_length()
    near = list(range(1, 1 + len(sizes)))
    orders = [near[i:] + near[:i] for i in range(len(sizes))]
    rest = list(range(1 + len(sizes), bits))
    x = halve(x, 0)
    groups = jnp.split(x, [sum(sizes[: i + 1]) for i in range(len(sizes) - 1)])
    for turn in range(len(near)):
        groups = [halve(g, order[turn]) for g, order in zip(groups, orders)]
    marks = [g.shape[0] for g in groups]
    x = jnp.concatenate(groups)
    for bit in rest:
        x = halve(x, bit)
    for bit in reversed(rest):
        x = double(x, bit)
    groups = jnp.split(x, [sum(marks[: i + 1]) for i in range(len(marks) - 1)])
    for turn in reversed(range(len(near))):
        groups = [double(g, order[turn]) for g, order in zip(groups, orders)]
    return double(jnp.concatenate(groups), 0)


def shifted(x, width):
    rows = x.shape[0]
    padded = jnp.pad(x, ((width // 2, width // 2), (0, 0)))
    return jnp.concatenate([padded[k : k + rows] for k in range(width)], axis=1)


def shards(
    mel, cotangent, lengths, w_first, w_mid, w_last, gain_hidden, bias_hidden, gain_last, bias_last
):
    batch, frames, mels = mel.shape
    width = w_first.shape[0]
    span = frames + 2 * EDGE
    rows = batch * span
    both = extend(jnp.concatenate([mel, cotangent], axis=2)).reshape(rows, 2 * mels)
    mel_ext, cot_ext = both[:, :mels], both[:, mels:]
    local = jnp.arange(span, dtype=jnp.int32) - EDGE
    position = lax.axis_index("tm") * frames + local
    live = (position[None, :] >= 0) & (position[None, :] < lengths[:, None])
    mask = live.astype(jnp.float32).reshape(rows, 1)
    inside = (local >= 0) & (local < frames)
    own = (live & inside[None, :]).astype(jnp.float32).reshape(rows, 1)
    local_count = jnp.sum(own)
    weights = [w_first, w_mid[0], w_mid[1], w_mid[2], w_last]
    gains = [gain_hidden[0], gain_hidden[1], gain_hidden[2], gain_hidden[3], gain_last]
    shifts = [bias_hidden[0], bias_hidden[1], bias_hidden[2], bias_hidden[3], bias_last]
    kept = []
    count = None
    x = mel_ext
    last_sums = None
    for layer in range(5):
        weight = weights[layer]
        x_wide = shifted(x, width)
        h = jnp.dot(x_wide, weight.reshape(-1, weight.shape[2]), precision=HIGH)
        masked = own * h
        sums = [jnp.sum(masked, axis=0), jnp.sum(masked * h, axis=0)]
        if layer == 0:
            sums.append(jnp.broadcast_to(local_count, sums[0].shape))
        if layer == 4:
            sums += [jnp.sum(own * cot_ext, axis=0), jnp.sum(masked * cot_ext, axis=0)]
        sums = all_sum(jnp.stack(sums))
        if layer == 0:
            count = sums[2, 0]
        mean = sums[0] / count
        rstd = lax.rsqrt(sums[1] / count - mean * mean + 1e-05)
        normed = (h - mean) * rstd
        z_value = normed * gains[layer] + shifts[layer]
        if layer < 4:
            active = jnp.tanh(z_value)
            x = mask * active
        else:
            active = None
            x = mask * z_value
            last_sums = (rstd * (sums[3] - mean * sums[2]), sums[2])
        kept.append((x_wide, normed, rstd, active))

    def unextend(block):
        return block.reshape(batch, span, mels)[:, EDGE : EDGE + frames]

    mel_after = mel + unextend(x)
    grad = cot_ext
    weight_grads = [None] * 5
    gain_grads = [None] * 5
    shift_grads = [None] * 5
    for layer in range(4, -1, -1):
        x_wide, normed, rstd, active = kept[layer]
        weight = weights[layer]
        gz = grad * mask
        if layer < 4:
            gz = gz * (1.0 - active * active)
            mine = own * gz
            sums = all_sum(jnp.stack([jnp.sum(mine * normed, axis=0), jnp.sum(mine, axis=0)]))
            d_gain, d_shift = sums[0], sums[1]
        else:
            d_gain, d_shift = last_sums
        gain_grads[layer] = d_gain
        shift_grads[layer] = d_shift
        d_pre = mask * rstd * gains[layer] * (gz - d_shift / count - normed * d_gain / count)
        weight_grads[layer] = jnp.dot(x_wide.T, own * d_pre, precision=HIGH)
        flipped = jnp.transpose(weight[::-1], (0, 2, 1)).reshape(-1, weight.shape[1])
        grad = jnp.dot(shifted(d_pre, width), flipped, precision=HIGH)
    grad_mel = cotangent + unextend(grad)
    weight_grads[3], weight_grads[4] = lax.psum((weight_grads[3], weight_grads[4]), AXES)
    weight_grads[2] = exchange_sum(weight_grads[2], [512, 384, 384])
    weight_grads[1] = exchange_sum(weight_grads[1], [512, 384, 384])
    first = weight_grads[0]
    padded = jnp.pad(first, ((0, -first.shape[0] % 512), (0, 0)))
    weight_grads[0] = exchange_sum(padded, [padded.shape[0] // 2])[: first.shape[0]]
    grad_w_mid = jnp.stack([weight_grads[i].reshape(w_mid.shape[1:]) for i in (1, 2, 3)])
    return (
        mel_after,
        grad_mel,
        weight_grads[0].reshape(w_first.shape),
        grad_w_mid,
        weight_grads[4].reshape(w_last.shape),
        jnp.stack(gain_grads[:4]),
        jnp.stack(shift_grads[:4]),
        gain_grads[4],
        shift_grads[4],
    )


def solution(mesh):
    return jax.shard_map(
        shards,
        mesh=mesh,
        in_specs=(P("dp", "tm", None), P("dp", "tm", None), P("dp")) + (P(),) * 7,
        out_specs=(P("dp", "tm", None), P("dp", "tm", None)) + (P(),) * 7,
        check_vma=False,
    )
```

```python
import functools

import jax
import jax.numpy as jnp
from jax import lax
from jax.experimental import pallas as pl
from jax.experimental.pallas import tpu as pltpu
from jax.sharding import PartitionSpec as P

AXES = ("dp", "tm")
EDGE = 24
PAD = 8
F32 = jnp.float32
BF16 = jnp.bfloat16
NN = ((1,), (0,))
NT = ((1,), (1,))
TN = ((0,), (0,))
WHOLE = pl.BlockSpec(memory_space=pltpu.VMEM)
FAR = pl.BlockSpec(memory_space=pltpu.HBM)
SCALARS = pl.BlockSpec(memory_space=pltpu.SMEM)


def split(value):
    high = value.astype(BF16)
    return high, (value - high.astype(F32)).astype(BF16)


def product(left, right, dims):
    def one(a, b):
        return lax.dot_general(a, b, (dims, ((), ())), preferred_element_type=F32)

    return one(left[0], right[0]) + (one(left[0], right[1]) + one(left[1], right[0]))


def sum_over_devices(ref):
    return jnp.sum(ref[...], axis=0)


def masks(meta_ref, shape, batch, span):
    rows, own = [], []
    for b in range(batch):
        local = lax.broadcasted_iota(jnp.int32, (span, shape[1]), 0) - EDGE
        position = local + meta_ref[batch]
        live = (position >= 0) & (position < meta_ref[b])
        rows.append(live)
        own.append(live & (local >= 0) & (local < span - 2 * EDGE))
    return jnp.concatenate(rows, axis=0), jnp.concatenate(own, axis=0)


def put_copies(ref, rows):
    ref[...] = jnp.broadcast_to(jnp.concatenate(rows, axis=0)[None], ref.shape)


def column_sum(value):
    return jnp.sum(value, axis=0, keepdims=True)


def fetch(refs, names):
    copies = {n: pltpu.make_async_copy(refs[n], refs[n + "_here"], refs["sem_" + n]) for n in names}
    for copy in copies.values():
        copy.start()

    def get(name):
        copies[name].wait()
        return refs[name + "_here"][...]

    return get


def fetch_scratch(arrays):
    scratch = {}
    for name, array in arrays.items():
        scratch[name + "_here"] = pltpu.VMEM(array.shape, F32)
        scratch["sem_" + name] = pltpu.SemaphoreType.DMA
    return scratch


def weight_copy(layer, refs, k):
    source = refs["w"] if layer is None else refs["w"].at[layer]
    return pltpu.make_async_copy(source.at[k], refs["w_here"].at[k], refs["arrived"].at[k])


def fetch_weights(layer, refs):
    for k in range(refs["w_here"].shape[0]):
        weight_copy(layer, refs, k).start()


def taps(out_ref, layer, refs, value, step, dims):
    rows = value.shape[0]
    w_ref, padded_ref, high_ref, low_ref = (refs[n] for n in ("w_here", "padded", "high", "low"))
    width = w_ref.shape[0]
    edge = jnp.zeros((PAD, value.shape[1]), F32)
    padded_ref[0:PAD, :] = edge
    padded_ref[PAD : PAD + rows, :] = value
    padded_ref[PAD + rows : PAD + rows + PAD, :] = edge
    for k in range(width):
        start = PAD + step * (k - width // 2)
        high_ref[k], low_ref[k] = split(padded_ref[start : start + rows, :])
    out_ref[...] = jnp.zeros(out_ref.shape, F32)

    def tap(k, carry):
        weight_copy(layer, refs, k).wait()
        out_ref[...] += product((high_ref[k], low_ref[k]), split(w_ref[k]), dims)
        return carry

    lax.fori_loop(0, width, tap, 0)


def tap_scratch(rows, dims, contracted):
    wide = (dims[0], rows, contracted)
    return dict(
        padded=pltpu.VMEM((rows + 2 * PAD, contracted), F32), high=pltpu.VMEM(wide, BF16), low=pltpu.VMEM(wide, BF16),
        w_here=pltpu.VMEM(dims, F32), arrived=pltpu.SemaphoreType.DMA((dims[0],)),
    )


def normalizer(sums, inverse):
    mean = sums[0:1] * inverse
    return mean, lax.rsqrt(sums[1:2] * inverse - mean * mean + 1e-05)


def first_forward(batch, refs):
    fetch_weights(None, refs)
    meta_ref, mel_ref, cot_ref, before_ref, after_ref, h_ref, copies_ref, mel_ext_ref, cot_ext_ref = (
        refs[n] for n in ("meta", "mel", "cot", "before", "after", "h", "copies", "mel_ext", "cot_ext")
    )
    frames = mel_ref.shape[1]
    span = frames + 2 * EDGE
    for b in range(batch):
        base = b * span
        for i, (ref, out) in enumerate(((mel_ref, mel_ext_ref), (cot_ref, cot_ext_ref))):
            out[base : base + EDGE, :] = before_ref[i, b]
            out[base + EDGE : base + EDGE + frames, :] = ref[b]
            out[base + EDGE + frames : base + span, :] = after_ref[i, b]
    taps(h_ref, None, refs, mel_ext_ref[...], 1, NN)
    h = h_ref[...]
    _, own = masks(meta_ref, h.shape, batch, span)
    h = jnp.where(own, h, 0.0)
    put_copies(copies_ref, [column_sum(h), column_sum(h * h), column_sum(own.astype(F32))])


def forward(batch, layer, last, refs):
    fetch_weights(layer, refs)
    meta_ref, h_in_ref, sums_ref, gain_ref, bias_ref, h_ref, copies_ref, x_ref, stats_ref = (
        refs[n] for n in ("meta", "h_in", "sums", "gain", "bias", "h", "copies", "x", "stats")
    )
    span = h_in_ref.shape[0] // batch
    sums = sum_over_devices(sums_ref)
    count = refs["count"][...] if "count" in refs else sums[2:3]
    mean, rstd = normalizer(sums, 1.0 / count)
    stats_ref[0:1, :] = mean
    stats_ref[1:2, :] = rstd
    stats_ref[2:3, :] = count
    h = h_in_ref[...]
    live, own = masks(meta_ref, h.shape, batch, span)
    x = jnp.where(live, jnp.tanh((h - mean) * rstd * gain_ref[...] + bias_ref[...]), 0.0)
    x_ref[...] = x
    taps(h_ref, layer, refs, x, 1, NT if last else NN)
    h = h_ref[...]
    _, own = masks(meta_ref, h.shape, batch, span)
    h = jnp.where(own, h, 0.0)
    sums = [column_sum(h), column_sum(h * h)]
    if last:
        cot = jnp.where(own, refs["cot"][...], 0.0)
        sums += [column_sum(cot), column_sum(h * cot)]
    put_copies(copies_ref, sums)


def backward(batch, layer, kind, refs):
    get = fetch(refs, ["h"])
    fetch_weights(layer, refs)
    get_below = None if kind == "first" else fetch(refs, ["x", "below_h"])
    meta_ref, sums_ref, h_ref, gz_ref, stats_ref, gain_ref = (
        refs[n] for n in ("meta", "sums", "h", "gz", "stats", "gain")
    )
    rows = h_ref.shape[0]
    span = rows // batch
    frames = span - 2 * EDGE
    channels = h_ref.shape[1]
    sums = sum_over_devices(sums_ref)
    inverse = 1.0 / stats_ref[2:3, :channels]
    if kind == "last":
        mean, rstd = normalizer(sums, inverse)
        shift = sums[2:3]
        gain = rstd * (sums[3:4] - mean * shift)
    else:
        mean, rstd = stats_ref[0:1, :], stats_ref[1:2, :]
        gain, shift = sums[0:1], sums[1:2]
    refs["param_grads"][0:1, :] = gain
    refs["param_grads"][1:2, :] = shift
    live, _ = masks(meta_ref, h_ref.shape, batch, span)
    normed = (get("h") - mean) * rstd
    if kind == "last":
        x = jnp.where(live, normed * gain_ref[...] + refs["bias"][...], 0.0)
        for b in range(batch):
            at = b * span + EDGE
            refs["mel_after"][b] = refs["mel"][b] + x[at : at + frames]
    gz = gz_ref[...]
    dh = rstd * gain_ref[...] * (gz - shift * inverse - normed * (gain * inverse))
    dh = jnp.where(live, dh, 0.0)
    refs["dh"][...] = dh
    e_ref = refs["e"]
    taps(e_ref, layer, refs, dh, -1, NN if kind == "last" else NT)
    if kind == "first":
        for b in range(batch):
            at = b * span + EDGE
            refs["grad_mel"][b] = refs["cot"][b] + e_ref[at : at + frames, :]
        return
    live, own = masks(meta_ref, e_ref.shape, batch, span)
    x = get_below("x")
    gz = jnp.where(live, e_ref[...] * (1.0 - x * x), 0.0)
    refs["gz_out"][...] = gz
    below = refs["below_stats"]
    normed = (get_below("below_h") - below[0:1, :]) * below[1:2, :]
    gz = jnp.where(own, gz, 0.0)
    put_copies(refs["copies"], [column_sum(gz * normed), column_sum(gz)])


def weight_gradient(batch, turned, refs):
    get = fetch(refs, ["x"])
    dh_ref, shifted_ref = refs["dh"], refs["shifted"]
    span = dh_ref.shape[0] // batch
    frames = span - 2 * EDGE
    width = shifted_ref.shape[0]
    dh = jnp.concatenate([dh_ref[b * span + EDGE : b * span + EDGE + frames, :] for b in range(batch)], axis=0)
    dh = split(dh.T if turned else dh)
    get("x")
    for k in range(width):
        for b in range(batch):
            start = b * span + EDGE + k - width // 2
            shifted_ref[k, b * frames : (b + 1) * frames] = refs["x_here"][start : start + frames, :]
    upper = refs["meta"][batch + 1] == 1

    def tap(k, carry):
        if turned:
            dw = product(dh, split(shifted_ref[k]), NN)
        else:
            dw = product(split(shifted_ref[k].T), dh, NN)
        if "whole" in refs:
            refs["whole"][k] = dw
        else:
            half = refs["mine"].shape[1]
            refs["mine"][k] = jnp.where(upper, dw[half:], dw[:half])
            refs["other"][k] = jnp.where(upper, dw[:half], dw[half:])
        return carry

    lax.fori_loop(0, width, tap, 0)


def place_whole(index, refs):
    copy = pltpu.make_async_copy(refs["value"], refs["out"].at[index], refs["sem"])
    copy.start()
    copy.wait()


def place(index, refs):
    meta_ref, mine_ref, other_ref, sems, out_ref = (refs[n] for n in ("meta", "mine", "other", "sems", "out"))
    half = mine_ref.shape[1]
    target = out_ref if index is None else out_ref.at[index]
    upper = meta_ref[meta_ref.shape[0] - 1]
    first = pltpu.make_async_copy(mine_ref, target.at[:, pl.ds(upper * half, half)], sems.at[0])
    second = pltpu.make_async_copy(other_ref, target.at[:, pl.ds((1 - upper) * half, half)], sems.at[1])
    first.start()
    second.start()
    first.wait()
    second.wait()


def shape(*dims):
    return jax.ShapeDtypeStruct(dims, F32)


def call(body, name, ins, outs, scratch, flops, far=("w",), far_outs=(), alias=None):
    names = list(ins) + list(outs) + list(scratch)

    def kernel(*refs):
        body(dict(zip(names, refs)))

    size = sum(4 * v.size for v in list(ins.values()) + list(outs.values()))
    results = pl.pallas_call(
        kernel,
        name=name,
        out_shape=list(outs.values()),
        in_specs=[SCALARS if n == "meta" else FAR if n in far else WHOLE for n in ins],
        out_specs=[FAR if n in far_outs else WHOLE for n in outs],
        input_output_aliases={} if alias is None else {list(ins).index(alias[0]): list(outs).index(alias[1])},
        scratch_shapes=list(scratch.values()),
        cost_estimate=pl.CostEstimate(flops=flops, bytes_accessed=size if flops else 0, transcendentals=0),
        compiler_params=pltpu.CompilerParams(vmem_limit_bytes=50 * 2**20),
    )(*ins.values())
    return dict(zip(outs, results))


def edges(mel, cotangent):
    count = lax.axis_size("tm")
    up = [(i, i + 1) for i in range(count - 1)]
    down = [(j, i) for i, j in up]
    low = lax.ppermute(jnp.stack([mel[:, -EDGE:], cotangent[:, -EDGE:]]), "tm", up)
    high = lax.ppermute(jnp.stack([mel[:, :EDGE], cotangent[:, :EDGE]]), "tm", down)
    return low, high


def to_all(copies):
    return lax.all_to_all(copies, AXES, 0, 0)


def swap(x, bit):
    devices = lax.axis_size(AXES)
    return lax.ppermute(x, AXES, [(i, i ^ (1 << bit)) for i in range(devices)])


def upper_half(bit):
    return ((lax.axis_index(AXES) >> bit) & 1) == 1


def halve(x, bit):
    half = x.shape[0] // 2
    upper = upper_half(bit)
    low, high = x[:half], x[half:]
    return jnp.where(upper, high, low) + swap(jnp.where(upper, low, high), bit)


def double(x, bit):
    upper = upper_half(bit)
    other = swap(x, bit)
    return jnp.concatenate([jnp.where(upper, other, x), jnp.where(upper, x, other)], axis=0)


def assemble(parts, sizes):
    rows = sum(p.shape[0] for p in parts)
    spare = sum(sizes) - rows
    parts = list(parts)
    if spare:
        parts.append(jnp.zeros((spare, parts[0].shape[1]), F32))
    groups, start = [], 0
    for size in sizes:
        pieces, at = [], 0
        for p in parts:
            low, high = max(start, at), min(start + size, at + p.shape[0])
            if low < high:
                pieces.append(p[low - at : high - at])
            at += p.shape[0]
        groups.append(pieces[0] if len(pieces) == 1 else jnp.concatenate(pieces))
        start += size
    return groups


class Exchange:
    def __init__(self, pairs, sizes):
        bits = (lax.axis_size(AXES) - 1).bit_length()
        near = list(range(1, 1 + len(sizes)))
        orders = [near[i:] + near[:i] for i in range(len(sizes))]
        rest = list(range(1 + len(sizes), bits))
        marks = [s >> len(near) for s in sizes]
        self.state = [m for m, _ in pairs] + [o for _, o in pairs]
        count = len(pairs)
        self.steps = [lambda s: assemble([m + swap(o, 0) for m, o in zip(s[:count], s[count:])], sizes)]
        for turn in range(len(near)):
            self.steps.append(lambda s, turn=turn: [halve(g, order[turn]) for g, order in zip(s, orders)])
        for i, bit in enumerate(rest):
            self.steps.append(lambda s, bit=bit: [halve(jnp.concatenate(s), bit)])
        for bit in reversed(rest):
            self.steps.append(lambda s, bit=bit: [double(s[0], bit)])
        for turn in reversed(range(len(near))):
            first = turn == len(near) - 1 and bool(rest)
            self.steps.append(
                lambda s, turn=turn, first=first: [
                    double(g, order[turn]) for g, order in zip(assemble(s, marks) if first else s, orders)
                ]
            )

        def finish(s):
            x = jnp.concatenate(s)
            return [x, swap(x, 0)]

        self.steps.append(finish)

    def advance(self):
        if self.steps:
            self.state = self.steps.pop(0)(self.state)


def tie(value, exchanges):
    states = [e.state for e in exchanges]
    value, states = lax.optimization_barrier((value, states))
    for e, state in zip(exchanges, states):
        e.state = state
    return value


def shards(
    mel, cotangent, lengths, w_first, w_mid, w_last, gain_hidden, bias_hidden, gain_last, bias_last
):
    batch, frames, mels = mel.shape
    width, channels = w_first.shape[0], w_first.shape[2]
    rows = batch * (frames + 2 * EDGE)
    devices = lax.axis_size(AXES)
    meta = jnp.concatenate([lengths, jnp.stack([lax.axis_index("tm") * frames, lax.axis_index(AXES) & 1]).astype(jnp.int32)])
    before, after = edges(mel, cotangent)
    weights = [(w_first, None, w_first.shape)]
    weights += [(w_mid, i, w_mid.shape[1:]) for i in range(w_mid.shape[0])]
    w_turned = w_last.transpose(0, 2, 1)
    weights += [(w_turned, None, w_turned.shape)]
    wide = [channels] * 4 + [mels]
    gains = [gain_hidden[i : i + 1] for i in range(4)] + [gain_last[None]]
    biases = [bias_hidden[i : i + 1] for i in range(4)] + [bias_last[None]]

    def work(dims):
        return 6 * rows * dims[0] * dims[1] * dims[2]

    out = call(
        functools.partial(first_forward, batch), "forward_first",
        dict(meta=meta, mel=mel, cot=cotangent, before=before, after=after, w=w_first),
        dict(h=shape(rows, channels), copies=shape(devices, 3, channels), mel_ext=shape(rows, mels), cot_ext=shape(rows, mels)),
        tap_scratch(rows, w_first.shape, mels), work(w_first.shape),
    )
    mel_ext, cot_ext = out["mel_ext"], out["cot_ext"]
    h = [out["h"]]
    x = [mel_ext]
    stats = []
    count = None
    gathered = to_all(out["copies"])
    for layer in range(1, 5):
        last = layer == 4
        weight, index, dims = weights[layer]
        ins = dict(meta=meta, h_in=h[-1], sums=gathered, gain=gains[layer - 1], bias=biases[layer - 1], w=weight)
        if count is not None:
            ins["count"] = count
        if last:
            ins["cot"] = cot_ext
        out = call(
            functools.partial(forward, batch, index, last), "forward",
            ins,
            dict(h=shape(rows, wide[layer]), copies=shape(devices, 4 if last else 2, wide[layer]),
                 x=shape(rows, channels), stats=shape(3, channels)),
            tap_scratch(rows, dims, channels), work(dims),
        )
        h.append(out["h"])
        x.append(out["x"])
        stats.append(out["stats"])
        if count is None:
            count = out["stats"][2:3]
        gathered = to_all(out["copies"])
    gz = cot_ext
    param_grads = [None] * 5
    exchanges = []
    for layer in range(4, -1, -1):
        kind = "last" if layer == 4 else "first" if layer == 0 else "inner"
        weight, index, dims = weights[layer]
        above, below = wide[layer], wide[layer - 1] if layer else mels
        ins = dict(meta=meta, sums=gathered, h=h[layer], gz=gz, stats=stats[min(layer, 3)], gain=gains[layer], w=weight)
        outs = dict(dh=shape(rows, above), param_grads=shape(2, above))
        scratch = dict(tap_scratch(rows, dims, above), e=pltpu.VMEM((rows, below), F32))
        far = dict(h=h[layer])
        if kind == "last":
            ins.update(bias=biases[layer], mel=mel)
            outs.update(mel_after=shape(*mel.shape))
        if kind == "first":
            ins.update(cot=cotangent)
            outs.update(grad_mel=shape(*mel.shape))
        else:
            ins.update(x=x[layer], below_h=h[layer - 1], below_stats=stats[layer - 1])
            far.update(x=x[layer], below_h=h[layer - 1])
            outs.update(gz_out=shape(rows, below), copies=shape(devices, 2, below))
        scratch.update(fetch_scratch(far))
        out = call(functools.partial(backward, batch, index, kind), "backward", ins, outs, scratch, 0, far=("w", *far))
        param_grads[layer] = out["param_grads"]
        if kind == "last":
            mel_after = out["mel_after"]
        if kind == "first":
            grad_mel = out["grad_mel"]
        else:
            gz = out["gz_out"]
            gathered = to_all(out["copies"])

        for e in exchanges:
            e.advance()
        dh = tie(out["dh"], exchanges)
        if layer >= 3:
            pieces = dict(whole=shape(*dims))
        else:
            pieces = dict(mine=shape(dims[0], dims[1] // 2, dims[2]), other=shape(dims[0], dims[1] // 2, dims[2]))
        pieces = call(
            functools.partial(weight_gradient, batch, kind == "last"), "weight_gradient",
            dict(meta=meta, x=x[layer], dh=dh), pieces,
            dict(shifted=pltpu.VMEM((width, batch * frames, below), F32), **fetch_scratch(dict(x=x[layer]))), 0, far=("x",),
        )
        for e in exchanges:
            e.advance()
        pieces = [v.reshape(-1, channels) if layer < 3 else v for v in pieces.values()]
        if layer == 4:
            held = pieces[0]
            gathered, held = lax.optimization_barrier((gathered, held))
        elif layer == 3:
            gathered, whole = lax.optimization_barrier((gathered, pieces[0]))
            summed = lax.psum((whole, held), AXES)
        elif layer == 2:
            tile = pieces[0].shape[0] // 10
            exchanges.append(Exchange([pieces], [4 * tile, 3 * tile, 3 * tile]))
            gathered = tie(gathered, exchanges)
        elif layer == 1:
            held = pieces
            gathered, held = lax.optimization_barrier((gathered, held))
            gathered = tie(gathered, exchanges)
        else:
            rows_all = held[0].shape[0] + pieces[0].shape[0]
            exchanges.append(Exchange([held, pieces], [-(-rows_all // 192) * 64] * 3))
    early, late = exchanges
    while late.steps:
        late.advance()
        early.advance()
        early.state, _ = lax.optimization_barrier((early.state, late.state))
    half = channels // 2
    mid = (width, half, channels)
    small = (width, mels // 2, channels)
    mid_rows, small_rows = width * half, width * mels // 2
    grad_w_mid = call(
        functools.partial(place_whole, 2), "place_whole", dict(value=summed[0]), dict(out=shape(*w_mid.shape)),
        dict(sem=pltpu.SemaphoreType.DMA), 0, far=(), far_outs=("out",),
    )["out"]
    for index, e in ((1, exchanges[0]), (0, exchanges[1])):
        grad_w_mid = call(
            functools.partial(place, index), "place",
            dict(meta=meta, mine=e.state[0][:mid_rows].reshape(mid), other=e.state[1][:mid_rows].reshape(mid), before=grad_w_mid),
            dict(out=shape(*w_mid.shape)), dict(sems=pltpu.SemaphoreType.DMA((2,))), 0,
            far=("before",), far_outs=("out",), alias=("before", "out"),
        )["out"]
    mine, other = (v[mid_rows : mid_rows + small_rows].reshape(small) for v in exchanges[1].state)
    upper = upper_half(0)
    grad_w_first = jnp.concatenate([jnp.where(upper, other, mine), jnp.where(upper, mine, other)], axis=1)
    return (
        mel_after,
        grad_mel,
        grad_w_first,
        grad_w_mid,
        summed[1].transpose(0, 2, 1),
        jnp.concatenate([p[0:1] for p in param_grads[:4]]),
        jnp.concatenate([p[1:2] for p in param_grads[:4]]),
        param_grads[4][0],
        param_grads[4][1],
    )


def solution(mesh):
    return jax.shard_map(
        shards,
        mesh=mesh,
        in_specs=(P("dp", "tm", None), P("dp", "tm", None), P("dp")) + (P(),) * 7,
        out_specs=(P("dp", "tm", None), P("dp", "tm", None)) + (P(),) * 7,
        check_vma=False,
    )
```

```python
import functools

import jax
import jax.numpy as jnp
from jax import lax
from jax.experimental import pallas as pl
from jax.experimental.pallas import tpu as pltpu
from jax.sharding import PartitionSpec as P

AXES = ("dp", "tm")
EDGE = 24
PAD = 8
F32 = jnp.float32
BF16 = jnp.bfloat16
NN = ((1,), (0,))
NT = ((1,), (1,))
TN = ((0,), (0,))
WHOLE = pl.BlockSpec(memory_space=pltpu.VMEM)
FAR = pl.BlockSpec(memory_space=pltpu.HBM)
SCALARS = pl.BlockSpec(memory_space=pltpu.SMEM)


def split(value):
    high = value.astype(BF16)
    return high, (value - high.astype(F32)).astype(BF16)


def product(left, right, dims):
    l = jnp.concatenate([left[0], left[0], left[1]], axis=dims[0][0])
    r = jnp.concatenate([right[0], right[1], right[0]], axis=dims[1][0])
    return lax.dot_general(l, r, (dims, ((), ())), preferred_element_type=F32)


def sum_over_devices(ref):
    return jnp.sum(ref[...], axis=0)


def masks(meta_ref, shape, batch, span):
    rows, own = [], []
    for b in range(batch):
        local = lax.broadcasted_iota(jnp.int32, (span, shape[1]), 0) - EDGE
        position = local + meta_ref[batch]
        live = (position >= 0) & (position < meta_ref[b])
        rows.append(live)
        own.append(live & (local >= 0) & (local < span - 2 * EDGE))
    return jnp.concatenate(rows, axis=0), jnp.concatenate(own, axis=0)


def put_copies(ref, rows):
    ref[...] = jnp.broadcast_to(jnp.concatenate(rows, axis=0)[None], ref.shape)


def column_sum(value):
    return jnp.sum(value, axis=0, keepdims=True)


def fetch(refs, names):
    copies = {n: pltpu.make_async_copy(refs[n], refs[n + "_here"], refs["sem_" + n]) for n in names}
    for copy in copies.values():
        copy.start()

    def get(name):
        copies[name].wait()
        return refs[name + "_here"][...]

    return get


def fetch_scratch(arrays):
    scratch = {}
    for name, array in arrays.items():
        scratch[name + "_here"] = pltpu.VMEM(array.shape, F32)
        scratch["sem_" + name] = pltpu.SemaphoreType.DMA
    return scratch


def weight_copy(layer, refs, k):
    source = refs["w"] if layer is None else refs["w"].at[layer]
    return pltpu.make_async_copy(source.at[k], refs["w_here"].at[k], refs["arrived"].at[k])


def fetch_weights(layer, refs):
    for k in range(refs["w_here"].shape[0]):
        weight_copy(layer, refs, k).start()


def taps(out_ref, layer, refs, value, step, dims):
    rows = value.shape[0]
    w_ref, padded_ref, high_ref, low_ref = (refs[n] for n in ("w_here", "padded", "high", "low"))
    width = w_ref.shape[0]
    edge = jnp.zeros((PAD, value.shape[1]), F32)
    padded_ref[0:PAD, :] = edge
    padded_ref[PAD : PAD + rows, :] = value
    padded_ref[PAD + rows : PAD + rows + PAD, :] = edge
    for k in range(width):
        start = PAD + step * (k - width // 2)
        high_ref[k], low_ref[k] = split(padded_ref[start : start + rows, :])
    out_ref[...] = jnp.zeros(out_ref.shape, F32)

    def tap(k, carry):
        weight_copy(layer, refs, k).wait()
        out_ref[...] += product((high_ref[k], low_ref[k]), split(w_ref[k]), dims)
        return carry

    lax.fori_loop(0, width, tap, 0, unroll=True)


def tap_scratch(rows, dims, contracted):
    wide = (dims[0], rows, contracted)
    return dict(
        padded=pltpu.VMEM((rows + 2 * PAD, contracted), F32), high=pltpu.VMEM(wide, BF16), low=pltpu.VMEM(wide, BF16),
        w_here=pltpu.VMEM(dims, F32), arrived=pltpu.SemaphoreType.DMA((dims[0],)),
    )


def normalizer(sums, inverse):
    mean = sums[0:1] * inverse
    return mean, lax.rsqrt(sums[1:2] * inverse - mean * mean + 1e-05)


def first_forward(batch, refs):
    fetch_weights(None, refs)
    meta_ref, mel_ref, cot_ref, before_ref, after_ref, h_ref, copies_ref, mel_ext_ref, cot_ext_ref = (
        refs[n] for n in ("meta", "mel", "cot", "before", "after", "h", "copies", "mel_ext", "cot_ext")
    )
    frames = mel_ref.shape[1]
    span = frames + 2 * EDGE
    for b in range(batch):
        base = b * span
        for i, (ref, out) in enumerate(((mel_ref, mel_ext_ref), (cot_ref, cot_ext_ref))):
            out[base : base + EDGE, :] = before_ref[i, b]
            out[base + EDGE : base + EDGE + frames, :] = ref[b]
            out[base + EDGE + frames : base + span, :] = after_ref[i, b]
    taps(h_ref, None, refs, mel_ext_ref[...], 1, NN)
    h = h_ref[...]
    _, own = masks(meta_ref, h.shape, batch, span)
    h = jnp.where(own, h, 0.0)
    put_copies(copies_ref, [column_sum(h), column_sum(h * h), column_sum(own.astype(F32))])


def forward(batch, layer, last, refs):
    fetch_weights(layer, refs)
    meta_ref, h_in_ref, sums_ref, gain_ref, bias_ref, h_ref, copies_ref, x_ref, stats_ref = (
        refs[n] for n in ("meta", "h_in", "sums", "gain", "bias", "h", "copies", "x", "stats")
    )
    span = h_in_ref.shape[0] // batch
    sums = sum_over_devices(sums_ref)
    count = refs["count"][...] if "count" in refs else sums[2:3]
    mean, rstd = normalizer(sums, 1.0 / count)
    stats_ref[0:1, :] = mean
    stats_ref[1:2, :] = rstd
    stats_ref[2:3, :] = count
    h = h_in_ref[...]
    live, own = masks(meta_ref, h.shape, batch, span)
    x = jnp.where(live, jnp.tanh((h - mean) * rstd * gain_ref[...] + bias_ref[...]), 0.0)
    x_ref[...] = x
    taps(h_ref, layer, refs, x, 1, NT if last else NN)
    h = h_ref[...]
    _, own = masks(meta_ref, h.shape, batch, span)
    h = jnp.where(own, h, 0.0)
    sums = [column_sum(h), column_sum(h * h)]
    if last:
        cot = jnp.where(own, refs["cot"][...], 0.0)
        sums += [column_sum(cot), column_sum(h * cot)]
    put_copies(copies_ref, sums)


def backward(batch, layer, kind, refs):
    get = fetch(refs, ["h"])
    fetch_weights(layer, refs)
    get_below = None if kind == "first" else fetch(refs, ["x", "below_h"])
    meta_ref, sums_ref, h_ref, gz_ref, stats_ref, gain_ref = (
        refs[n] for n in ("meta", "sums", "h", "gz", "stats", "gain")
    )
    rows = h_ref.shape[0]
    span = rows // batch
    frames = span - 2 * EDGE
    channels = h_ref.shape[1]
    sums = sum_over_devices(sums_ref)
    inverse = 1.0 / stats_ref[2:3, :channels]
    if kind == "last":
        mean, rstd = normalizer(sums, inverse)
        shift = sums[2:3]
        gain = rstd * (sums[3:4] - mean * shift)
    else:
        mean, rstd = stats_ref[0:1, :], stats_ref[1:2, :]
        gain, shift = sums[0:1], sums[1:2]
    refs["param_grads"][0:1, :] = gain
    refs["param_grads"][1:2, :] = shift
    live, _ = masks(meta_ref, h_ref.shape, batch, span)
    normed = (get("h") - mean) * rstd
    if kind == "last":
        x = jnp.where(live, normed * gain_ref[...] + refs["bias"][...], 0.0)
        for b in range(batch):
            at = b * span + EDGE
            refs["mel_after"][b] = refs["mel"][b] + x[at : at + frames]
    gz = gz_ref[...]
    dh = rstd * gain_ref[...] * (gz - shift * inverse - normed * (gain * inverse))
    dh = jnp.where(live, dh, 0.0)
    refs["dh"][...] = dh
    e_ref = refs["e"]
    taps(e_ref, layer, refs, dh, -1, NN if kind == "last" else NT)
    if kind == "first":
        for b in range(batch):
            at = b * span + EDGE
            refs["grad_mel"][b] = refs["cot"][b] + e_ref[at : at + frames, :]
        return
    live, own = masks(meta_ref, e_ref.shape, batch, span)
    x = get_below("x")
    gz = jnp.where(live, e_ref[...] * (1.0 - x * x), 0.0)
    refs["gz_out"][...] = gz
    below = refs["below_stats"]
    normed = (get_below("below_h") - below[0:1, :]) * below[1:2, :]
    gz = jnp.where(own, gz, 0.0)
    put_copies(refs["copies"], [column_sum(gz * normed), column_sum(gz)])


def weight_gradient(batch, turned, refs):
    get = fetch(refs, ["x"])
    dh_ref, shifted_ref = refs["dh"], refs["shifted"]
    span = dh_ref.shape[0] // batch
    frames = span - 2 * EDGE
    width = shifted_ref.shape[0]
    dh = jnp.concatenate([dh_ref[b * span + EDGE : b * span + EDGE + frames, :] for b in range(batch)], axis=0)
    dh = split(dh.T if turned else dh)
    get("x")
    for k in range(width):
        for b in range(batch):
            start = b * span + EDGE + k - width // 2
            shifted_ref[k, b * frames : (b + 1) * frames] = refs["x_here"][start : start + frames, :]
    upper = refs["meta"][batch + 1] == 1

    def tap(k, carry):
        if turned:
            dw = product(dh, split(shifted_ref[k]), NN)
        else:
            dw = product(split(shifted_ref[k].T), dh, NN)
        if "whole" in refs:
            refs["whole"][k] = dw
        else:
            half = refs["mine"].shape[1]
            refs["mine"][k] = jnp.where(upper, dw[half:], dw[:half])
            refs["other"][k] = jnp.where(upper, dw[:half], dw[half:])
        return carry

    lax.fori_loop(0, width, tap, 0, unroll=True)


def place_whole(index, refs):
    copy = pltpu.make_async_copy(refs["value"], refs["out"].at[index], refs["sem"])
    copy.start()
    copy.wait()


def place(index, refs):
    meta_ref, out_ref = refs["meta"], refs["out"]
    width, half = out_ref.shape[1], out_ref.shape[2] // 2
    upper = meta_ref[meta_ref.shape[0] - 1]
    copies = []
    for i, (name, at) in enumerate((("mine", upper), ("other", 1 - upper))):
        for k in range(width):
            source = refs[name].at[pl.ds(k * half, half)]
            copies.append(pltpu.make_async_copy(source, out_ref.at[index, k, pl.ds(at * half, half)], refs["sems"].at[i, k]))
    for copy in copies:
        copy.start()
    for copy in copies:
        copy.wait()


def shape(*dims):
    return jax.ShapeDtypeStruct(dims, F32)


def call(body, name, ins, outs, scratch, flops, far=("w",), far_outs=(), alias=None):
    names = list(ins) + list(outs) + list(scratch)

    def kernel(*refs):
        body(dict(zip(names, refs)))

    size = sum(4 * v.size for v in list(ins.values()) + list(outs.values()))
    results = pl.pallas_call(
        kernel,
        name=name,
        out_shape=list(outs.values()),
        in_specs=[SCALARS if n == "meta" else FAR if n in far else WHOLE for n in ins],
        out_specs=[FAR if n in far_outs else WHOLE for n in outs],
        input_output_aliases={} if alias is None else {list(ins).index(alias[0]): list(outs).index(alias[1])},
        scratch_shapes=list(scratch.values()),
        cost_estimate=pl.CostEstimate(flops=flops, bytes_accessed=size if flops else 0, transcendentals=0),
        compiler_params=pltpu.CompilerParams(vmem_limit_bytes=50 * 2**20),
    )(*ins.values())
    return dict(zip(outs, results))


def edges(mel, cotangent):
    count = lax.axis_size("tm")
    up = [(i, i + 1) for i in range(count - 1)]
    down = [(j, i) for i, j in up]
    low = lax.ppermute(jnp.stack([mel[:, -EDGE:], cotangent[:, -EDGE:]]), "tm", up)
    high = lax.ppermute(jnp.stack([mel[:, :EDGE], cotangent[:, :EDGE]]), "tm", down)
    return low, high


def to_all(copies):
    return lax.all_to_all(copies, AXES, 0, 0)


def swap(x, bit):
    devices = lax.axis_size(AXES)
    return lax.ppermute(x, AXES, [(i, i ^ (1 << bit)) for i in range(devices)])


def upper_half(bit):
    return ((lax.axis_index(AXES) >> bit) & 1) == 1


def halve(x, bit):
    half = x.shape[0] // 2
    upper = upper_half(bit)
    low, high = x[:half], x[half:]
    return jnp.where(upper, high, low) + swap(jnp.where(upper, low, high), bit)


def double(x, bit):
    upper = upper_half(bit)
    other = swap(x, bit)
    return jnp.concatenate([jnp.where(upper, other, x), jnp.where(upper, x, other)], axis=0)


def assemble(parts, sizes):
    rows = sum(p.shape[0] for p in parts)
    spare = sum(sizes) - rows
    parts = list(parts)
    if spare:
        parts.append(jnp.zeros((spare, parts[0].shape[1]), F32))
    groups, start = [], 0
    for size in sizes:
        pieces, at = [], 0
        for p in parts:
            low, high = max(start, at), min(start + size, at + p.shape[0])
            if low < high:
                pieces.append(p[low - at : high - at])
            at += p.shape[0]
        groups.append(pieces[0] if len(pieces) == 1 else jnp.concatenate(pieces))
        start += size
    return groups


class Exchange:
    def __init__(self, pairs, sizes):
        bits = (lax.axis_size(AXES) - 1).bit_length()
        near = list(range(1, 1 + len(sizes)))
        orders = [near[i:] + near[:i] for i in range(len(sizes))]
        rest = list(range(1 + len(sizes), bits))
        marks = [s >> len(near) for s in sizes]
        self.state = [m for m, _ in pairs] + [o for _, o in pairs]
        count = len(pairs)
        self.steps = [lambda s: assemble([m + swap(o, 0) for m, o in zip(s[:count], s[count:])], sizes)]
        for turn in range(len(near)):
            self.steps.append(lambda s, turn=turn: [halve(g, order[turn]) for g, order in zip(s, orders)])
        for i, bit in enumerate(rest):
            self.steps.append(lambda s, bit=bit: [halve(jnp.concatenate(s), bit)])
        for bit in reversed(rest):
            self.steps.append(lambda s, bit=bit: [double(s[0], bit)])
        for turn in reversed(range(len(near))):
            first = turn == len(near) - 1 and bool(rest)
            self.steps.append(
                lambda s, turn=turn, first=first: [
                    double(g, order[turn]) for g, order in zip(assemble(s, marks) if first else s, orders)
                ]
            )

        def finish(s):
            x = jnp.concatenate(s)
            return [x, swap(x, 0)]

        self.steps.append(finish)

    def advance(self):
        if self.steps:
            self.state = self.steps.pop(0)(self.state)


def tie(value, exchanges):
    states = [e.state for e in exchanges]
    value, states = lax.optimization_barrier((value, states))
    for e, state in zip(exchanges, states):
        e.state = state
    return value


def shards(
    mel, cotangent, lengths, w_first, w_mid, w_last, gain_hidden, bias_hidden, gain_last, bias_last
):
    batch, frames, mels = mel.shape
    width, channels = w_first.shape[0], w_first.shape[2]
    rows = batch * (frames + 2 * EDGE)
    devices = lax.axis_size(AXES)
    meta = jnp.concatenate([lengths, jnp.stack([lax.axis_index("tm") * frames, lax.axis_index(AXES) & 1]).astype(jnp.int32)])
    before, after = edges(mel, cotangent)
    weights = [(w_first, None, w_first.shape)]
    weights += [(w_mid, i, w_mid.shape[1:]) for i in range(w_mid.shape[0])]
    w_turned = w_last.transpose(0, 2, 1)
    weights += [(w_turned, None, w_turned.shape)]
    wide = [channels] * 4 + [mels]
    gains = [gain_hidden[i : i + 1] for i in range(4)] + [gain_last[None]]
    biases = [bias_hidden[i : i + 1] for i in range(4)] + [bias_last[None]]

    def work(dims):
        return 6 * rows * dims[0] * dims[1] * dims[2]

    out = call(
        functools.partial(first_forward, batch), "forward_first",
        dict(meta=meta, mel=mel, cot=cotangent, before=before, after=after, w=w_first),
        dict(h=shape(rows, channels), copies=shape(devices, 3, channels), mel_ext=shape(rows, mels), cot_ext=shape(rows, mels)),
        tap_scratch(rows, w_first.shape, mels), work(w_first.shape),
    )
    mel_ext, cot_ext = out["mel_ext"], out["cot_ext"]
    h = [out["h"]]
    x = [mel_ext]
    stats = []
    count = None
    gathered = to_all(out["copies"])
    for layer in range(1, 5):
        last = layer == 4
        weight, index, dims = weights[layer]
        ins = dict(meta=meta, h_in=h[-1], sums=gathered, gain=gains[layer - 1], bias=biases[layer - 1], w=weight)
        if count is not None:
            ins["count"] = count
        if last:
            ins["cot"] = cot_ext
        out = call(
            functools.partial(forward, batch, index, last), "forward",
            ins,
            dict(h=shape(rows, wide[layer]), copies=shape(devices, 4 if last else 2, wide[layer]),
                 x=shape(rows, channels), stats=shape(3, channels)),
            tap_scratch(rows, dims, channels), work(dims),
        )
        h.append(out["h"])
        x.append(out["x"])
        stats.append(out["stats"])
        if count is None:
            count = out["stats"][2:3]
        gathered = to_all(out["copies"])
    gz = cot_ext
    param_grads = [None] * 5
    exchanges = []
    for layer in range(4, -1, -1):
        kind = "last" if layer == 4 else "first" if layer == 0 else "inner"
        weight, index, dims = weights[layer]
        above, below = wide[layer], wide[layer - 1] if layer else mels
        ins = dict(meta=meta, sums=gathered, h=h[layer], gz=gz, stats=stats[min(layer, 3)], gain=gains[layer], w=weight)
        outs = dict(dh=shape(rows, above), param_grads=shape(2, above))
        scratch = dict(tap_scratch(rows, dims, above), e=pltpu.VMEM((rows, below), F32))
        far = dict(h=h[layer])
        if kind == "last":
            ins.update(bias=biases[layer], mel=mel)
            outs.update(mel_after=shape(*mel.shape))
        if kind == "first":
            ins.update(cot=cotangent)
            outs.update(grad_mel=shape(*mel.shape))
        else:
            ins.update(x=x[layer], below_h=h[layer - 1], below_stats=stats[layer - 1])
            far.update(x=x[layer], below_h=h[layer - 1])
            outs.update(gz_out=shape(rows, below), copies=shape(devices, 2, below))
        scratch.update(fetch_scratch(far))
        out = call(functools.partial(backward, batch, index, kind), "backward", ins, outs, scratch, 8 * work(dims), far=("w", *far))
        param_grads[layer] = out["param_grads"]
        if kind == "last":
            mel_after = out["mel_after"]
        if kind == "first":
            grad_mel = out["grad_mel"]
        else:
            gz = out["gz_out"]
            gathered = to_all(out["copies"])

        for e in exchanges:
            e.advance()
        dh = tie(out["dh"], exchanges)
        if layer >= 3:
            pieces = dict(whole=shape(*dims))
        else:
            pieces = dict(mine=shape(dims[0], dims[1] // 2, dims[2]), other=shape(dims[0], dims[1] // 2, dims[2]))
        pieces = call(
            functools.partial(weight_gradient, batch, kind == "last"), "weight_gradient",
            dict(meta=meta, x=x[layer], dh=dh), pieces,
            dict(shifted=pltpu.VMEM((width, batch * frames, below), F32), **fetch_scratch(dict(x=x[layer]))), 8 * work(dims), far=("x",),
        )
        for e in exchanges:
            e.advance()
        pieces = [v.reshape(-1, channels) if layer < 3 else v for v in pieces.values()]
        if layer == 4:
            held = pieces[0]
            gathered, held = lax.optimization_barrier((gathered, held))
        elif layer == 3:
            gathered, whole = lax.optimization_barrier((gathered, pieces[0]))
            summed = lax.psum((whole, held), AXES)
        elif layer == 2:
            tile = pieces[0].shape[0] // 10
            exchanges.append(Exchange([pieces], [4 * tile, 3 * tile, 3 * tile]))
            gathered = tie(gathered, exchanges)
        elif layer == 1:
            held = pieces
            gathered, held = lax.optimization_barrier((gathered, held))
            gathered = tie(gathered, exchanges)
        else:
            rows_all = held[0].shape[0] + pieces[0].shape[0]
            exchanges.append(Exchange([held, pieces], [-(-rows_all // 192) * 64] * 3))
    early, late = exchanges

    def placed(index, e, before):
        ins = dict(meta=meta, mine=e.state[0], other=e.state[1])
        if before is not None:
            ins["before"] = before
        return call(
            functools.partial(place, index), "place", ins, dict(out=shape(*w_mid.shape)), dict(sems=pltpu.SemaphoreType.DMA((2, width))), 0,
            far=("before",), far_outs=("out",), alias=None if before is None else ("before", "out"),
        )["out"]

    while late.steps:
        late.advance()
        if early.steps:
            early.advance()
            early.state, _ = lax.optimization_barrier((early.state, late.state))
    half = channels // 2
    small = (width, mels // 2, channels)
    mid_rows, small_rows = width * half, width * mels // 2
    grad_w_mid = call(
        functools.partial(place_whole, 2), "place_whole", dict(value=summed[0]), dict(out=shape(*w_mid.shape)),
        dict(sem=pltpu.SemaphoreType.DMA), 0, far=(), far_outs=("out",),
    )["out"]
    grad_w_mid = placed(1, early, grad_w_mid)
    grad_w_mid = placed(0, late, grad_w_mid)
    mine, other = (v[mid_rows : mid_rows + small_rows].reshape(small) for v in exchanges[1].state)
    upper = upper_half(0)
    grad_w_first = jnp.concatenate([jnp.where(upper, other, mine), jnp.where(upper, mine, other)], axis=1)
    return (
        mel_after,
        grad_mel,
        grad_w_first,
        grad_w_mid,
        summed[1].transpose(0, 2, 1),
        jnp.concatenate([p[0:1] for p in param_grads[:4]]),
        jnp.concatenate([p[1:2] for p in param_grads[:4]]),
        param_grads[4][0],
        param_grads[4][1],
    )


def solution(mesh):
    return jax.shard_map(
        shards,
        mesh=mesh,
        in_specs=(P("dp", "tm", None), P("dp", "tm", None), P("dp")) + (P(),) * 7,
        out_specs=(P("dp", "tm", None), P("dp", "tm", None)) + (P(),) * 7,
        check_vma=False,
    )
```

```python
import functools

import jax
import jax.numpy as jnp
from jax import lax
from jax.experimental import pallas as pl
from jax.experimental.pallas import tpu as pltpu
from jax.sharding import PartitionSpec as P

AXES = ("dp", "tm")
EDGE = 24
PAD = 8
F32 = jnp.float32
BF16 = jnp.bfloat16
NN = ((1,), (0,))
NT = ((1,), (1,))
TN = ((0,), (0,))
WHOLE = pl.BlockSpec(memory_space=pltpu.VMEM)
FAR = pl.BlockSpec(memory_space=pltpu.HBM)
SCALARS = pl.BlockSpec(memory_space=pltpu.SMEM)


def split(value):
    high = value.astype(BF16)
    return high, (value - high.astype(F32)).astype(BF16)


def product(left, right, dims):
    l = jnp.concatenate([left[0], left[0], left[1]], axis=dims[0][0])
    r = jnp.concatenate([right[0], right[1], right[0]], axis=dims[1][0])
    return lax.dot_general(l, r, (dims, ((), ())), preferred_element_type=F32)


def sum_over_devices(ref):
    return jnp.sum(ref[...], axis=0)


def masks(meta_ref, shape, batch, span):
    rows, own = [], []
    for b in range(batch):
        local = lax.broadcasted_iota(jnp.int32, (span, shape[1]), 0) - EDGE
        position = local + meta_ref[batch]
        live = (position >= 0) & (position < meta_ref[b])
        rows.append(live)
        own.append(live & (local >= 0) & (local < span - 2 * EDGE))
    return jnp.concatenate(rows, axis=0), jnp.concatenate(own, axis=0)


def put_copies(ref, rows):
    ref[...] = jnp.broadcast_to(jnp.concatenate(rows, axis=0)[None], ref.shape)


def column_sum(value):
    return jnp.sum(value, axis=0, keepdims=True)


def fetch(refs, names):
    copies = {n: pltpu.make_async_copy(refs[n], refs[n + "_here"], refs["sem_" + n]) for n in names}
    for copy in copies.values():
        copy.start()

    def get(name):
        copies[name].wait()
        return refs[name + "_here"][...]

    return get


def fetch_scratch(arrays):
    scratch = {}
    for name, array in arrays.items():
        scratch[name + "_here"] = pltpu.VMEM(array.shape, F32)
        scratch["sem_" + name] = pltpu.SemaphoreType.DMA
    return scratch


def weight_copy(layer, refs, k):
    source = refs["w"] if layer is None else refs["w"].at[layer]
    return pltpu.make_async_copy(source.at[k], refs["w_here"].at[k], refs["arrived"].at[k])


def fetch_weights(layer, refs):
    for k in range(refs["w_here"].shape[0]):
        weight_copy(layer, refs, k).start()


def taps(out_ref, layer, refs, value, step, dims):
    rows = value.shape[0]
    w_ref, padded_ref, high_ref, low_ref = (refs[n] for n in ("w_here", "padded", "high", "low"))
    width = w_ref.shape[0]
    edge = jnp.zeros((PAD, value.shape[1]), F32)
    padded_ref[0:PAD, :] = edge
    padded_ref[PAD : PAD + rows, :] = value
    padded_ref[PAD + rows : PAD + rows + PAD, :] = edge
    for k in range(width):
        start = PAD + step * (k - width // 2)
        high_ref[k], low_ref[k] = split(padded_ref[start : start + rows, :])
    out_ref[...] = jnp.zeros(out_ref.shape, F32)

    def tap(k, carry):
        weight_copy(layer, refs, k).wait()
        out_ref[...] += product((high_ref[k], low_ref[k]), split(w_ref[k]), dims)
        return carry

    lax.fori_loop(0, width, tap, 0, unroll=True)


def tap_scratch(rows, dims, contracted):
    wide = (dims[0], rows, contracted)
    return dict(
        padded=pltpu.VMEM((rows + 2 * PAD, contracted), F32), high=pltpu.VMEM(wide, BF16), low=pltpu.VMEM(wide, BF16),
        w_here=pltpu.VMEM(dims, F32), arrived=pltpu.SemaphoreType.DMA((dims[0],)),
    )


def normalizer(sums, inverse):
    mean = sums[0:1] * inverse
    return mean, lax.rsqrt(sums[1:2] * inverse - mean * mean + 1e-05)


def first_forward(batch, refs):
    fetch_weights(None, refs)
    meta_ref, mel_ref, cot_ref, before_ref, after_ref, h_ref, copies_ref, mel_ext_ref, cot_ext_ref = (
        refs[n] for n in ("meta", "mel", "cot", "before", "after", "h", "copies", "mel_ext", "cot_ext")
    )
    frames = mel_ref.shape[1]
    span = frames + 2 * EDGE
    for b in range(batch):
        base = b * span
        for i, (ref, out) in enumerate(((mel_ref, mel_ext_ref), (cot_ref, cot_ext_ref))):
            out[base : base + EDGE, :] = before_ref[i, b]
            out[base + EDGE : base + EDGE + frames, :] = ref[b]
            out[base + EDGE + frames : base + span, :] = after_ref[i, b]
    taps(h_ref, None, refs, mel_ext_ref[...], 1, NN)
    h = h_ref[...]
    _, own = masks(meta_ref, h.shape, batch, span)
    h = jnp.where(own, h, 0.0)
    put_copies(copies_ref, [column_sum(h), column_sum(h * h), column_sum(own.astype(F32))])


def forward(batch, layer, last, refs):
    fetch_weights(layer, refs)
    meta_ref, h_in_ref, sums_ref, gain_ref, bias_ref, h_ref, copies_ref, x_ref, stats_ref = (
        refs[n] for n in ("meta", "h_in", "sums", "gain", "bias", "h", "copies", "x", "stats")
    )
    span = h_in_ref.shape[0] // batch
    sums = sum_over_devices(sums_ref)
    count = refs["count"][...] if "count" in refs else sums[2:3]
    mean, rstd = normalizer(sums, 1.0 / count)
    stats_ref[0:1, :] = mean
    stats_ref[1:2, :] = rstd
    stats_ref[2:3, :] = count
    h = h_in_ref[...]
    live, own = masks(meta_ref, h.shape, batch, span)
    x = jnp.where(live, jnp.tanh((h - mean) * rstd * gain_ref[...] + bias_ref[...]), 0.0)
    x_ref[...] = x
    taps(h_ref, layer, refs, x, 1, NT if last else NN)
    h = h_ref[...]
    _, own = masks(meta_ref, h.shape, batch, span)
    h = jnp.where(own, h, 0.0)
    sums = [column_sum(h), column_sum(h * h)]
    if last:
        cot = jnp.where(own, refs["cot"][...], 0.0)
        sums += [column_sum(cot), column_sum(h * cot)]
    put_copies(copies_ref, sums)


def backward(batch, layer, kind, refs):
    get = fetch(refs, ["h"])
    fetch_weights(layer, refs)
    get_below = None if kind == "first" else fetch(refs, ["x", "below_h"])
    meta_ref, sums_ref, h_ref, gz_ref, stats_ref, gain_ref = (
        refs[n] for n in ("meta", "sums", "h", "gz", "stats", "gain")
    )
    rows = h_ref.shape[0]
    span = rows // batch
    frames = span - 2 * EDGE
    channels = h_ref.shape[1]
    sums = sum_over_devices(sums_ref)
    inverse = 1.0 / stats_ref[2:3, :channels]
    if kind == "last":
        mean, rstd = normalizer(sums, inverse)
        shift = sums[2:3]
        gain = rstd * (sums[3:4] - mean * shift)
    else:
        mean, rstd = stats_ref[0:1, :], stats_ref[1:2, :]
        gain, shift = sums[0:1], sums[1:2]
    refs["param_grads"][0:1, :] = gain
    refs["param_grads"][1:2, :] = shift
    live, _ = masks(meta_ref, h_ref.shape, batch, span)
    normed = (get("h") - mean) * rstd
    if kind == "last":
        x = jnp.where(live, normed * gain_ref[...] + refs["bias"][...], 0.0)
        for b in range(batch):
            at = b * span + EDGE
            refs["mel_after"][b] = refs["mel"][b] + x[at : at + frames]
    gz = gz_ref[...]
    dh = rstd * gain_ref[...] * (gz - shift * inverse - normed * (gain * inverse))
    dh = jnp.where(live, dh, 0.0)
    refs["dh"][...] = dh
    e_ref = refs["e"]
    taps(e_ref, layer, refs, dh, -1, NN if kind == "last" else NT)
    if kind == "first":
        for b in range(batch):
            at = b * span + EDGE
            refs["grad_mel"][b] = refs["cot"][b] + e_ref[at : at + frames, :]
        return
    live, own = masks(meta_ref, e_ref.shape, batch, span)
    x = get_below("x")
    gz = jnp.where(live, e_ref[...] * (1.0 - x * x), 0.0)
    refs["gz_out"][...] = gz
    below = refs["below_stats"]
    normed = (get_below("below_h") - below[0:1, :]) * below[1:2, :]
    gz = jnp.where(own, gz, 0.0)
    put_copies(refs["copies"], [column_sum(gz * normed), column_sum(gz)])


def weight_gradient(batch, turned, refs):
    get = fetch(refs, ["x"])
    dh_ref, shifted_ref = refs["dh"], refs["shifted"]
    span = dh_ref.shape[0] // batch
    frames = span - 2 * EDGE
    width = shifted_ref.shape[0]
    dh = jnp.concatenate([dh_ref[b * span + EDGE : b * span + EDGE + frames, :] for b in range(batch)], axis=0)
    dh = split(dh.T if turned else dh)
    get("x")
    for k in range(width):
        for b in range(batch):
            start = b * span + EDGE + k - width // 2
            shifted_ref[k, b * frames : (b + 1) * frames] = refs["x_here"][start : start + frames, :]
    upper = refs["meta"][batch + 1] == 1

    def tap(k, carry):
        if turned:
            dw = product(dh, split(shifted_ref[k]), NN)
        else:
            dw = product(split(shifted_ref[k].T), dh, NN)
        if "whole" in refs:
            refs["whole"][k] = dw
        else:
            half = refs["mine"].shape[1]
            refs["mine"][k] = jnp.where(upper, dw[half:], dw[:half])
            refs["other"][k] = jnp.where(upper, dw[:half], dw[half:])
        return carry

    lax.fori_loop(0, width, tap, 0, unroll=True)


def place_whole(index, refs):
    copy = pltpu.make_async_copy(refs["value"], refs["out"].at[index], refs["sem"])
    copy.start()
    copy.wait()


def place(index, refs):
    meta_ref, out_ref = refs["meta"], refs["out"]
    width, half = out_ref.shape[1], out_ref.shape[2] // 2
    upper = meta_ref[meta_ref.shape[0] - 1]
    copies = []
    for i, (name, at) in enumerate((("mine", upper), ("other", 1 - upper))):
        for k in range(width):
            source = refs[name].at[pl.ds(k * half, half)]
            copies.append(pltpu.make_async_copy(source, out_ref.at[index, k, pl.ds(at * half, half)], refs["sems"].at[i, k]))
    for copy in copies:
        copy.start()
    for copy in copies:
        copy.wait()


def shape(*dims):
    return jax.ShapeDtypeStruct(dims, F32)


def call(body, name, ins, outs, scratch, flops, far=("w",), far_outs=(), alias=None):
    names = list(ins) + list(outs) + list(scratch)

    def kernel(*refs):
        body(dict(zip(names, refs)))

    size = sum(4 * v.size for v in list(ins.values()) + list(outs.values()))
    results = pl.pallas_call(
        kernel,
        name=name,
        out_shape=list(outs.values()),
        in_specs=[SCALARS if n == "meta" else FAR if n in far else WHOLE for n in ins],
        out_specs=[FAR if n in far_outs else WHOLE for n in outs],
        input_output_aliases={} if alias is None else {list(ins).index(alias[0]): list(outs).index(alias[1])},
        scratch_shapes=list(scratch.values()),
        cost_estimate=pl.CostEstimate(flops=flops, bytes_accessed=size if flops else 0, transcendentals=0),
        compiler_params=pltpu.CompilerParams(vmem_limit_bytes=50 * 2**20),
    )(*ins.values())
    return dict(zip(outs, results))


def edges(mel, cotangent):
    count = lax.axis_size("tm")
    up = [(i, i + 1) for i in range(count - 1)]
    down = [(j, i) for i, j in up]
    low = lax.ppermute(jnp.stack([mel[:, -EDGE:], cotangent[:, -EDGE:]]), "tm", up)
    high = lax.ppermute(jnp.stack([mel[:, :EDGE], cotangent[:, :EDGE]]), "tm", down)
    return low, high


def to_all(copies):
    return lax.all_to_all(copies, AXES, 0, 0)


def swap(x, bit):
    devices = lax.axis_size(AXES)
    return lax.ppermute(x, AXES, [(i, i ^ (1 << bit)) for i in range(devices)])


def upper_half(bit):
    return ((lax.axis_index(AXES) >> bit) & 1) == 1


def halve(x, bit):
    half = x.shape[0] // 2
    upper = upper_half(bit)
    low, high = x[:half], x[half:]
    return jnp.where(upper, high, low) + swap(jnp.where(upper, low, high), bit)


def double(x, bit):
    upper = upper_half(bit)
    other = swap(x, bit)
    return jnp.concatenate([jnp.where(upper, other, x), jnp.where(upper, x, other)], axis=0)


def assemble(parts, sizes):
    rows = sum(p.shape[0] for p in parts)
    spare = sum(sizes) - rows
    parts = list(parts)
    if spare:
        parts.append(jnp.zeros((spare, parts[0].shape[1]), F32))
    groups, start = [], 0
    for size in sizes:
        pieces, at = [], 0
        for p in parts:
            low, high = max(start, at), min(start + size, at + p.shape[0])
            if low < high:
                pieces.append(p[low - at : high - at])
            at += p.shape[0]
        groups.append(pieces[0] if len(pieces) == 1 else jnp.concatenate(pieces))
        start += size
    return groups


class Exchange:
    def __init__(self, pairs, sizes):
        bits = (lax.axis_size(AXES) - 1).bit_length()
        near = list(range(1, 1 + len(sizes)))
        orders = [near[i:] + near[:i] for i in range(len(sizes))]
        rest = list(range(1 + len(sizes), bits))
        marks = [s >> len(near) for s in sizes]
        self.state = [m for m, _ in pairs] + [o for _, o in pairs]
        count = len(pairs)
        self.steps = [lambda s: assemble([m + swap(o, 0) for m, o in zip(s[:count], s[count:])], sizes)]
        for turn in range(len(near)):
            self.steps.append(lambda s, turn=turn: [halve(g, order[turn]) for g, order in zip(s, orders)])
        for i, bit in enumerate(rest):
            self.steps.append(lambda s, bit=bit: [halve(jnp.concatenate(s), bit)])
        for bit in reversed(rest):
            self.steps.append(lambda s, bit=bit: [double(s[0], bit)])
        for turn in reversed(range(len(near))):
            first = turn == len(near) - 1 and bool(rest)
            self.steps.append(
                lambda s, turn=turn, first=first: [
                    double(g, order[turn]) for g, order in zip(assemble(s, marks) if first else s, orders)
                ]
            )

        def finish(s):
            x = jnp.concatenate(s)
            return [x, swap(x, 0)]

        self.steps.append(finish)

    def advance(self):
        if self.steps:
            self.state = self.steps.pop(0)(self.state)


def tie(value, exchanges):
    states = [e.state for e in exchanges]
    value, states = lax.optimization_barrier((value, states))
    for e, state in zip(exchanges, states):
        e.state = state
    return value


def shards(
    mel, cotangent, lengths, w_first, w_mid, w_last, gain_hidden, bias_hidden, gain_last, bias_last
):
    batch, frames, mels = mel.shape
    width, channels = w_first.shape[0], w_first.shape[2]
    rows = batch * (frames + 2 * EDGE)
    devices = lax.axis_size(AXES)
    meta = jnp.concatenate([lengths, jnp.stack([lax.axis_index("tm") * frames, lax.axis_index(AXES) & 1]).astype(jnp.int32)])
    before, after = edges(mel, cotangent)
    weights = [(w_first, None, w_first.shape)]
    weights += [(w_mid, i, w_mid.shape[1:]) for i in range(w_mid.shape[0])]
    w_turned = w_last.transpose(0, 2, 1)
    weights += [(w_turned, None, w_turned.shape)]
    wide = [channels] * 4 + [mels]
    gains = [gain_hidden[i : i + 1] for i in range(4)] + [gain_last[None]]
    biases = [bias_hidden[i : i + 1] for i in range(4)] + [bias_last[None]]

    def work(dims):
        return 6 * rows * dims[0] * dims[1] * dims[2]

    out = call(
        functools.partial(first_forward, batch), "forward_first",
        dict(meta=meta, mel=mel, cot=cotangent, before=before, after=after, w=w_first),
        dict(h=shape(rows, channels), copies=shape(devices, 3, channels), mel_ext=shape(rows, mels), cot_ext=shape(rows, mels)),
        tap_scratch(rows, w_first.shape, mels), work(w_first.shape),
    )
    mel_ext, cot_ext = out["mel_ext"], out["cot_ext"]
    h = [out["h"]]
    x = [mel_ext]
    stats = []
    count = None
    gathered = to_all(out["copies"])
    for layer in range(1, 5):
        last = layer == 4
        weight, index, dims = weights[layer]
        ins = dict(meta=meta, h_in=h[-1], sums=gathered, gain=gains[layer - 1], bias=biases[layer - 1], w=weight)
        if count is not None:
            ins["count"] = count
        if last:
            ins["cot"] = cot_ext
        out = call(
            functools.partial(forward, batch, index, last), "forward",
            ins,
            dict(h=shape(rows, wide[layer]), copies=shape(devices, 4 if last else 2, wide[layer]),
                 x=shape(rows, channels), stats=shape(3, channels)),
            tap_scratch(rows, dims, channels), work(dims),
        )
        h.append(out["h"])
        x.append(out["x"])
        stats.append(out["stats"])
        if count is None:
            count = out["stats"][2:3]
        gathered = to_all(out["copies"])
    gz = cot_ext
    param_grads = [None] * 5
    exchanges = []
    for layer in range(4, -1, -1):
        kind = "last" if layer == 4 else "first" if layer == 0 else "inner"
        weight, index, dims = weights[layer]
        above, below = wide[layer], wide[layer - 1] if layer else mels
        ins = dict(meta=meta, sums=gathered, h=h[layer], gz=gz, stats=stats[min(layer, 3)], gain=gains[layer], w=weight)
        outs = dict(dh=shape(rows, above), param_grads=shape(2, above))
        scratch = dict(tap_scratch(rows, dims, above), e=pltpu.VMEM((rows, below), F32))
        far = dict(h=h[layer])
        if kind == "last":
            ins.update(bias=biases[layer], mel=mel)
            outs.update(mel_after=shape(*mel.shape))
        if kind == "first":
            ins.update(cot=cotangent)
            outs.update(grad_mel=shape(*mel.shape))
        else:
            ins.update(x=x[layer], below_h=h[layer - 1], below_stats=stats[layer - 1])
            far.update(x=x[layer], below_h=h[layer - 1])
            outs.update(gz_out=shape(rows, below), copies=shape(devices, 2, below))
        scratch.update(fetch_scratch(far))
        out = call(functools.partial(backward, batch, index, kind), "backward", ins, outs, scratch, 8 * work(dims), far=("w", *far))
        param_grads[layer] = out["param_grads"]
        if kind == "last":
            mel_after = out["mel_after"]
        if kind == "first":
            grad_mel = out["grad_mel"]
        else:
            gz = out["gz_out"]
            gathered = to_all(out["copies"])

        for e in exchanges:
            e.advance()
        dh = tie(out["dh"], exchanges)
        if layer >= 3:
            pieces = dict(whole=shape(*dims))
        else:
            pieces = dict(mine=shape(dims[0], dims[1] // 2, dims[2]), other=shape(dims[0], dims[1] // 2, dims[2]))
        pieces = call(
            functools.partial(weight_gradient, batch, kind == "last"), "weight_gradient",
            dict(meta=meta, x=x[layer], dh=dh), pieces,
            dict(shifted=pltpu.VMEM((width, batch * frames, below), F32), **fetch_scratch(dict(x=x[layer]))), 8 * work(dims), far=("x",),
        )
        for e in exchanges:
            e.advance()
        pieces = [v.reshape(-1, channels) if layer < 3 else v for v in pieces.values()]
        if layer == 4:
            held = pieces[0]
            gathered, held = lax.optimization_barrier((gathered, held))
        elif layer == 3:
            gathered, whole = lax.optimization_barrier((gathered, pieces[0]))
            summed = lax.psum((whole, held), AXES)
        elif layer == 2:
            tile = pieces[0].shape[0] // 10
            exchanges.append(Exchange([pieces], [4 * tile, 3 * tile, 3 * tile]))
            gathered = tie(gathered, exchanges)
        elif layer == 1:
            held = pieces
            gathered, held = lax.optimization_barrier((gathered, held))
            gathered = tie(gathered, exchanges)
        else:
            rows_all = held[0].shape[0] + pieces[0].shape[0]
            exchanges.append(Exchange([held, pieces], [-(-rows_all // 192) * 64] * 3))
    early, late = exchanges

    def placed(index, e, before):
        ins = dict(meta=meta, mine=e.state[0], other=e.state[1])
        if before is not None:
            ins["before"] = before
        return call(
            functools.partial(place, index), "place", ins, dict(out=shape(*w_mid.shape)), dict(sems=pltpu.SemaphoreType.DMA((2, width))), 0,
            far=("before",), far_outs=("out",), alias=None if before is None else ("before", "out"),
        )["out"]

    while late.steps:
        late.advance()
        if early.steps and len(late.steps) <= len(early.steps) + 1:
            early.advance()
            early.state, _ = lax.optimization_barrier((early.state, late.state))
    while early.steps:
        early.advance()
    half = channels // 2
    small = (width, mels // 2, channels)
    mid_rows, small_rows = width * half, width * mels // 2
    grad_w_mid = call(
        functools.partial(place_whole, 2), "place_whole", dict(value=summed[0]), dict(out=shape(*w_mid.shape)),
        dict(sem=pltpu.SemaphoreType.DMA), 0, far=(), far_outs=("out",),
    )["out"]
    grad_w_mid = placed(1, early, grad_w_mid)
    grad_w_mid = placed(0, late, grad_w_mid)
    mine, other = (v[mid_rows : mid_rows + small_rows].reshape(small) for v in exchanges[1].state)
    upper = upper_half(0)
    grad_w_first = jnp.concatenate([jnp.where(upper, other, mine), jnp.where(upper, mine, other)], axis=1)
    return (
        mel_after,
        grad_mel,
        grad_w_first,
        grad_w_mid,
        summed[1].transpose(0, 2, 1),
        jnp.concatenate([p[0:1] for p in param_grads[:4]]),
        jnp.concatenate([p[1:2] for p in param_grads[:4]]),
        param_grads[4][0],
        param_grads[4][1],
    )


def solution(mesh):
    return jax.shard_map(
        shards,
        mesh=mesh,
        in_specs=(P("dp", "tm", None), P("dp", "tm", None), P("dp")) + (P(),) * 7,
        out_specs=(P("dp", "tm", None), P("dp", "tm", None)) + (P(),) * 7,
        check_vma=False,
    )
```
